128 devices in a mesh: row: 8 (over z, core), col: 8 (over y_hi, x), freq: 2 (over y_lo).
Axes of the slice: x: 4, y: 4 (y_hi: 2, y_lo: 2; y = y_hi * 2 + y_lo), z: 4, core: 2. Of those that a mesh axis runs over, the one named last changes fastest.
Arguments:
- pair_elements: bfloat16 [2, 1024, 8192], P(None, ('row', 'freq'), 'col'), may hold values from -1.59375 to 1.59375
- transitions: int32 [3, 1024], replicated, may hold values from 0 to 63, as said below
- energies: float32 [16, 64], replicated, may hold values from -3 to 3
- occupations: int32 [16, 64], replicated, may hold values from 0 to 2
- frequencies: float32 [4], P('freq'), may hold values from 0.2 to 2
Outputs:
- chi_zero: float32 [4, 2, 8192, 8192], P('freq', None, 'row', 'col')
The draws below stay inside these ranges and needn't reach their ends.
Inputs may be any that keep to these rules, and one draw needn't show every extreme that they name: transitions[0] is a k-point below 16, transitions[1] a valence band below 32, transitions[2] a conduction band of 32 to 63.
All inputs are finite; a program needn't handle non-finite values.
Results may differ from the reference program's by a relative error of at most 0.0028.
Values may be sent and summed in bfloat16 or wider, within the bound.
A program may use at most 128 MiB of HBM per device.

```python
import math
import jax
import jax.numpy as jnp
from jax import lax

NPW = 8192
NFREQ = 4
TRANSITION_COUNT = 1024
NKPT = 16
NBAND = 64
VALENCE_LIMIT = 32


def draw_transitions(key, part):
    kpoint_key, valence_key, conduction_key = jax.random.split(jax.random.fold_in(key, 17), 3)
    kpoint = jax.random.randint(kpoint_key, (TRANSITION_COUNT,), 0, NKPT, dtype=jnp.int32)
    valence_bands = jax.random.randint(valence_key, (TRANSITION_COUNT,), 0, VALENCE_LIMIT, dtype=jnp.int32)
    conduction = jax.random.randint(conduction_key, (TRANSITION_COUNT,), VALENCE_LIMIT, NBAND, dtype=jnp.int32)
    valence_bands = valence_bands.at[0].set(0)
    conduction = conduction.at[0].set(NBAND - 1)
    return jnp.stack([kpoint, valence_bands, conduction], 0)


def plant(values, rng, low, high):
    dims = values.shape
    place = [jax.random.randint(jax.random.fold_in(rng, axis), (), 0, dims[axis]) for axis in range(len(dims))]
    values = values.at[tuple(place)].set(low)
    longest = dims.index(max(dims))
    place[longest] = (place[longest] + 1) % dims[longest]
    return values.at[tuple(place)].set(high)


def block_scale(own_key, extent, cuts, least, largest):
    factor_of, own = 1.0, jax.random.fold_in(own_key, 6)
    for position, blocks in cuts:
        draws = jnp.exp(jax.random.uniform(jax.random.fold_in(own, position), (blocks,), jnp.float32, least / len(cuts), largest / len(cuts)))
        factor_of = factor_of * jnp.repeat(draws, extent[position] // blocks).reshape([-1 if axis == position else 1 for axis in range(len(extent))])
    return factor_of


def bell_draw(key, shape, scale, bound, shards=(), kind=jnp.bfloat16):
    drawn = scale * jax.random.normal(key, shape, jnp.float32)
    if shards:
        drawn = drawn * block_scale(key, shape, shards, -0.22, 0.18)
    return jnp.clip(drawn, -bound, bound).astype(kind)


def setup_inputs(seed: int = 0) -> dict:
    key_of = jax.random.split(jax.random.key(seed), 6)
    return {
        "pair_elements": bell_draw(key_of[0], (2, TRANSITION_COUNT, NPW), 0.2, 1.59375, ((1, 16), (2, 8))),
        "transitions": draw_transitions(jax.random.fold_in(key_of[5], 71), 0),
        "energies": jnp.clip(jax.random.uniform(key_of[2], (NKPT, NBAND), jnp.float32, -3.0, 3.0), -3.0, 3.0),
        "occupations": plant(jax.random.randint(key_of[3], (NKPT, NBAND), 0, 3), jax.random.fold_in(key_of[3], 1), 0, 2).astype(jnp.int32),
        "frequencies": jnp.clip(jnp.exp(math.log(2.0) - 2.3025851 * jax.random.uniform(key_of[4], (NFREQ,), jnp.float32) ** block_scale(key_of[4], (NFREQ,), ((0, 2),), -0.2, 0.2)), 0.2, 2.0),
    }


def weights(transitions, energies, occupations, frequencies):
    kpoint = transitions[0]
    valence_bands = transitions[1]
    conduction = transitions[2]
    gap = energies[kpoint, conduction] - energies[kpoint, valence_bands]
    filled = (occupations[kpoint, valence_bands] - occupations[kpoint, conduction]).astype(jnp.float32)
    return (filled[None, :] * 2.0 * gap[None, :]) / (gap[None, :] * gap[None, :] + frequencies[:, None] * frequencies[:, None])


def reference(pair_elements, transitions, energies, occupations, frequencies):
    weight = weights(transitions, energies, occupations, frequencies)
    right_both = jnp.concatenate([pair_elements[0], pair_elements[1]], 0).astype(jnp.float32)

    def single_frequency(column):
        scaled = (pair_elements.astype(jnp.float32) * column[None, :, None]).astype(jnp.bfloat16).astype(jnp.float32)
        real_left = jnp.concatenate([scaled[0], scaled[1]], 0)
        imag_left = jnp.concatenate([scaled[1], -scaled[0]], 0)
        real_component = jnp.dot(real_left.T, right_both, precision=lax.Precision.HIGHEST)
        imag_part = jnp.dot(imag_left.T, right_both, precision=lax.Precision.HIGHEST)
        return jnp.stack([real_component, imag_part], 0)

    return lax.map(single_frequency, weight)
```

```python
import functools

import jax
import jax.numpy as jnp
from jax import lax
from jax.experimental import pallas as pl
from jax.experimental.pallas import tpu as pltpu
from jax.sharding import PartitionSpec as P

MESH = pl.DeviceIdType.MESH
SHIFT = (0, 1, 3, 2)
A1, A2, A3, A4, B1, B2, B3, B4 = range(0, 16, 2)


def where_am_i():
    row, col, low = lax.axis_index("row"), lax.axis_index("col"), lax.axis_index("freq")
    return col % 4, 2 * (col // 4) + low, row // 2, row % 2


def device(x, y, z, core):
    return (2 * (z % 4) + core, 4 * ((y % 4) // 2) + x % 4, y % 2)


def slot_of(y, z):
    delta = (y + 8 - 2 * (z // 2)) % 4
    return 2 * (delta // 2) + (delta + delta // 2) % 2


def gather_kernel(pair, rowp, colp, own_sem, s_send, s_recv, r_send, r_recv, c_send, c_recv, b_send, b_recv):
    x, y, z, core = where_am_i()
    low = y % 2
    half = pair.shape[2] // 2
    diagonal = (2 * z + core == 4 * (y // 2) + x) & (core == 0)
    target_z, target_core = 2 * (y // 2) + x // 2, x % 2
    target_y = (y + 4 + core * (2 * low - 1)) % 4
    mine = 2 * core + low
    partner = 2 * core + 1 - low
    xm, xp = (x + 3) % 4, (x + 1) % 4
    s0, sm, sp = slot_of(y, z), slot_of(y + 3, z), slot_of(y + 1, z)
    to_xp, to_xm = device(x + 1, y, z, core), device(x + 3, y, z, core)
    to_yp, to_ym = device(x, y + 1, z, core), device(x, y + 3, z, core)
    to_zp, to_zm = device(x, y, z + 1, core), device(x, y, z + 3, core)
    to_sibling = device(x, y, z, 1 - core)
    to_partner = device(x, y + 1 - 2 * low + 4, z, core)

    delta = (y + 8 - 2 * (z // 2)) % 4
    from_core, from_low = delta // 2, (delta + delta // 2) % 2
    from_x, from_y = 2 * (z % 2) + core, 2 * (z // 2) + from_low

    barrier = pltpu.get_barrier_semaphore()
    for there in (to_xp, to_xm, to_yp, to_ym, to_zp, to_zm, to_sibling):
        pl.semaphore_signal(barrier, inc=1, device_id=there, device_id_type=MESH)
    for q in range(4):
        @pl.when(jnp.logical_not(diagonal & (x == q)))
        def _():
            pl.semaphore_signal(
                barrier, inc=1, device_id=device(q, target_y, target_z, target_core), device_id_type=MESH
            )

        @pl.when(jnp.logical_not(diagonal & (z == q)))
        def _():
            pl.semaphore_signal(
                barrier, inc=1, device_id=device(from_x, from_y, q, from_core), device_id_type=MESH
            )
    pl.semaphore_wait(barrier, 15 - 2 * diagonal.astype(jnp.int32))

    sent = []

    def send(src, dst, sems, slot, there):
        copy = pltpu.make_async_remote_copy(
            src_ref=src, dst_ref=dst, send_sem=sems[0].at[slot], recv_sem=sems[1].at[slot],
            device_id=there, device_id_type=MESH,
        )
        copy.start()
        sent.append(copy)
        return copy

    rows, cols, both = (r_send, r_recv), (c_send, c_recv), (b_send, b_recv)

    def sibling(round_, slot, index):
        ref = colp.at[round_, :, slot]
        return send(ref, ref, both, index, to_sibling)

    own = pltpu.make_async_copy(pair, colp.at[0, :, mine], own_sem)
    own.start()
    c_part = send(pair, colp.at[0, :, mine], cols, 0, to_partner)
    shift = (z + 4 - target_z) % 4
    target_round = shift + (shift == 2).astype(jnp.int32) - (shift == 3).astype(jnp.int32)
    scatter = []
    for q in range(4):
        src = pair.at[:, pl.ds(16 * q, 16), :]
        dst = rowp.at[target_round, :, mine, q]
        remote = pltpu.make_async_remote_copy(
            src_ref=src, dst_ref=dst, send_sem=s_send.at[q], recv_sem=s_recv.at[target_round],
            device_id=device(q, target_y, target_z, target_core), device_id_type=MESH,
        )
        local = pltpu.make_async_copy(src, dst, s_recv.at[target_round])
        here = diagonal & (x == q)

        @pl.when(here)
        def _():
            local.start()

        @pl.when(jnp.logical_not(here))
        def _():
            remote.start()

        scatter.append((here, remote))
    c_zp = send(pair, colp.at[2, :, mine], cols, 1, to_zp)
    c_zm = send(pair, colp.at[1, :, mine], cols, 2, to_zm)
    s_own = send(pair, colp.at[0, :, mine], both, 0, to_sibling)
    waits = [s_own]

    gather = {}

    def step(stage, j):
        def ref(part, *index):
            return rowp.at[(j, part) + index]

        def go(name, ref, there):
            gather[j, name] = send(ref, ref, rows, 16 * j + name, there)

        def arrived(*names):
            for name in names:
                gather[j, name].wait_recv()
                gather[j, name + 1].wait_recv()

        if stage == 0:
            mine_ref = rowp.at[j, :, s0, x]
            pltpu.make_async_copy(mine_ref, mine_ref, s_recv.at[j]).wait()
            go(A1, ref(0, s0, x), to_xp)
            go(A1 + 1, ref(0, s0, x), to_xm)
            go(B1, ref(1, s0, x), to_yp)
            go(B1 + 1, ref(1, s0, x), to_ym)
        if stage == 1:
            first, second = pl.ds(0, half), pl.ds(half, half)
            arrived(A1)
            go(A2, ref(0, s0, xm, slice(None), first), to_xp)
            go(A2 + 1, ref(0, s0, xp, slice(None), second), to_xm)
            arrived(B1)
            go(B2, ref(1, sm, x, slice(None), first), to_yp)
            go(B2 + 1, ref(1, sp, x, slice(None), second), to_ym)
        if stage == 2:
            arrived(A2)
            go(A3, ref(0, s0), to_yp)
            go(A3 + 1, ref(0, s0), to_ym)
            arrived(B2)
            go(B3, ref(1, slice(None), x), to_xp)
            go(B3 + 1, ref(1, slice(None), x), to_xm)
        if stage == 3:
            arrived(A3)
            go(A4, ref(0, sm, pl.ds(0, 2)), to_yp)
            go(A4 + 1, ref(0, sp, pl.ds(2, 2)), to_ym)
            arrived(B3)
            go(B4, ref(1, pl.ds(0, 2), xm), to_xp)
            go(B4 + 1, ref(1, pl.ds(2, 2), xp), to_xm)
        if stage == 4:
            arrived(A4, B4)

    step(0, 0)
    step(0, 1)
    step(1, 0)
    step(0, 2)
    step(1, 1)
    step(2, 0)
    c_part.wait_recv()
    ref = colp.at[0, :, partner]
    c_zp2 = send(ref, colp.at[2, :, partner], cols, 3, to_zp)
    c_zm2 = send(ref, colp.at[1, :, partner], cols, 4, to_zm)
    waits.append(sibling(0, partner, 1))
    step(0, 3)
    step(1, 2)
    step(2, 1)
    step(3, 0)
    c_zp.wait_recv()
    c_far = send(colp.at[2, :, mine], colp.at[3, :, mine], cols, 5, to_zp)
    waits.append(sibling(2, mine, 2))
    c_zm.wait_recv()
    waits.append(sibling(1, mine, 3))
    step(1, 3)
    step(2, 2)
    step(3, 1)
    step(4, 0)
    c_zm2.wait_recv()
    c_far2 = send(colp.at[1, :, partner], colp.at[3, :, partner], cols, 6, to_zm)
    waits.append(sibling(1, partner, 4))
    c_zp2.wait_recv()
    waits.append(sibling(2, partner, 5))
    step(2, 3)
    step(3, 2)
    step(4, 1)
    c_far.wait_recv()
    waits.append(sibling(3, mine, 6))
    c_far2.wait_recv()
    waits.append(sibling(3, partner, 7))
    step(3, 3)
    step(4, 2)
    step(4, 3)
    for copy in waits:
        copy.wait_recv()
    own.wait()
    for copy in sent:
        copy.wait_send()
    for here, remote in scatter:
        @pl.when(jnp.logical_not(here))
        def _():
            remote.wait_send()


def find_weights(transitions, energies, occupations, frequencies, weight):
    count = transitions.shape[1]
    bands, points = energies.shape
    kpoint, valence, conduction = transitions[0:1, :], transitions[1:2, :], transitions[2:3, :]
    pick = (lax.broadcasted_iota(jnp.int32, (points, count), 0) == kpoint).astype(jnp.float32)
    band = lax.broadcasted_iota(jnp.int32, (bands, count), 0)

    def of(table):
        values = jnp.dot(table, pick, precision=lax.Precision.HIGHEST, preferred_element_type=jnp.float32)

        def one(which):
            return jnp.sum(jnp.where(band == which, values, 0.0), axis=0, keepdims=True)

        return one(valence), one(conduction)

    low, high = of(energies[...])
    gap = high - low
    below, above = of(occupations[...].astype(jnp.float32))
    filled = below - above
    for f in range(weight.shape[0]):
        frequency = frequencies[f]
        weight[f : f + 1, :] = filled * 2.0 * gap / (gap * gap + frequency * frequency)


def compute_kernel(rowp, colp, transitions, energies, occupations, frequencies, out, weight):
    z = where_am_i()[2]

    @pl.when(pl.program_id(0) == 0)
    def _():
        find_weights(transitions, energies, occupations, frequencies, weight)

    block = rowp.shape[-1]
    right = colp[...].reshape(-1, colp.shape[-1])
    lefts = [
        rowp[j, part].reshape(-1, block).T.astype(jnp.float32) for j in range(4) for part in range(2)
    ]
    for f in range(out.shape[0]):
        real, imag = [], []
        for j in range(4):
            depth = lefts[0].shape[1]
            start = pl.multiple_of(((z + SHIFT[j]) % 4) * depth, depth)
            w = weight[f : f + 1, pl.ds(start, depth)]
            first = (lefts[2 * j] * w).astype(jnp.bfloat16)
            second = (lefts[2 * j + 1] * w).astype(jnp.bfloat16)
            real += [first, second]
            imag += [second, -first]
        for part, pieces in enumerate((real, imag)):
            out[f, part] = jnp.dot(
                jnp.concatenate(pieces, axis=1), right, preferred_element_type=jnp.float32
            )


def body(pair_elements, transitions, energies, occupations, frequencies):
    width = pair_elements.shape[2]
    dma = pltpu.SemaphoreType.DMA
    rowp, colp = pl.pallas_call(
        gather_kernel,
        out_shape=(
            jax.ShapeDtypeStruct((4, 2, 4, 4, 16, width), jnp.bfloat16),
            jax.ShapeDtypeStruct((4, 2, 4, 64, width), jnp.bfloat16),
        ),
        in_specs=[pl.BlockSpec(memory_space=pltpu.VMEM)],
        out_specs=[pl.BlockSpec(memory_space=pltpu.VMEM)] * 2,
        scratch_shapes=[
            dma, dma((4,)), dma((4,)), dma((64,)), dma((64,)), dma((7,)), dma((7,)), dma((8,)), dma((8,)),
        ],
        compiler_params=pltpu.CompilerParams(collective_id=0, has_side_effects=True),
    )(pair_elements)
    block = 256
    count = transitions.shape[1]
    return pl.pallas_call(
        compute_kernel,
        grid=(width // block,),
        out_shape=jax.ShapeDtypeStruct((2, 2, width, width), jnp.float32),
        in_specs=[
            pl.BlockSpec((4, 2, 4, 4, 16, block), lambda i: (0, 0, 0, 0, 0, i)),
            pl.BlockSpec((4, 2, 4, 64, width), lambda i: (0, 0, 0, 0, 0), pipeline_mode=pl.Buffered(1)),
            pl.BlockSpec((3, count), lambda i: (0, 0)),
            pl.BlockSpec((64, 16), lambda i: (0, 0)),
            pl.BlockSpec((64, 16), lambda i: (0, 0)),
            pl.BlockSpec(memory_space=pltpu.SMEM),
        ],
        out_specs=pl.BlockSpec((2, 2, block, width), lambda i: (0, 0, i, 0)),
        scratch_shapes=[pltpu.VMEM((2, count), jnp.float32)],
        compiler_params=pltpu.CompilerParams(vmem_limit_bytes=48 * 2**20),
    )(rowp, colp, transitions, energies.T, occupations.T, frequencies)


def solution(mesh):
    in_specs = (P(None, ("row", "freq"), "col"), P(), P(), P(), P("freq"))
    out_specs = P("freq", None, "row", "col")
    return jax.shard_map(body, mesh=mesh, in_specs=in_specs, out_specs=out_specs, check_vma=False)
```

```python
import functools

import jax
import jax.numpy as jnp
from jax import lax
from jax.experimental import pallas as pl
from jax.experimental.pallas import tpu as pltpu
from jax.sharding import PartitionSpec as P

MESH = pl.DeviceIdType.MESH
ORDER = (
    (0, 0), (0, 1), (1, 0), (0, 2), (1, 1), (2, 0), ("c", 0), (0, 3), (1, 2), (2, 1), (3, 0), ("c", 1), (1, 3),
    (2, 2), (3, 1), (4, 0), ("c", 2), ("k", 0), (2, 3), (3, 2), ("k", 1), (4, 1), ("c", 3), ("k", 2), (3, 3), ("k", 3),
    (4, 2), ("k", 4), ("k", 5), (4, 3),
)

TILE = 256
SHIFT = (0, 1, 3, 2)
A1, A2, A3, A4, B1, B2, B3, B4 = range(0, 16, 2)


def where_am_i():
    row, col, low = lax.axis_index("row"), lax.axis_index("col"), lax.axis_index("freq")
    return col % 4, 2 * (col // 4) + low, row // 2, row % 2


def device(x, y, z, core):
    return (2 * (z % 4) + core, 4 * ((y % 4) // 2) + x % 4, y % 2)


def slot_of(y, z):
    delta = (y + 8 - 2 * (z // 2)) % 4
    return 2 * (delta // 2) + (delta + delta // 2) % 2


def gather_kernel(
    pair, transitions, energies, occupations, frequencies, rowp, colp, weight, total, own_sem, s_send, s_recv, r_send, r_recv, c_send, c_recv,
    b_send, b_recv,
):
    x, y, z, core = where_am_i()
    low = y % 2
    half = pair.shape[2] // 2
    diagonal = (2 * z + core == 4 * (y // 2) + x) & (core == 0)
    target_z, target_core = 2 * (y // 2) + x // 2, x % 2
    target_y = (y + 4 + core * (2 * low - 1)) % 4
    mine = 2 * core + low
    partner = 2 * core + 1 - low
    xm, xp = (x + 3) % 4, (x + 1) % 4
    y_pair, y_next = y + 1 - 2 * low, y + 3 + 2 * low
    s0, s_pair, s_next = slot_of(y, z), slot_of(y_pair, z), slot_of(y_next, z)
    to_partner, to_next = device(x, y_pair, z, core), device(x, y_next, z, core)
    to_xp, to_xm = device(x + 1, y, z, core), device(x + 3, y, z, core)
    to_zp, to_zm = device(x, y, z + 1, core), device(x, y, z + 3, core)
    to_sibling = device(x, y, z, 1 - core)

    delta = (y + 8 - 2 * (z // 2)) % 4
    from_core, from_low = delta // 2, (delta + delta // 2) % 2
    from_x, from_y = 2 * (z % 2) + core, 2 * (z // 2) + from_low

    barrier = pltpu.get_barrier_semaphore()
    for there in (to_xp, to_xm, to_partner, to_next, to_zp, to_zm, to_sibling):
        pl.semaphore_signal(barrier, inc=1, device_id=there, device_id_type=MESH)
    for q in range(4):
        @pl.when(jnp.logical_not(diagonal & (x == q)))
        def _():
            pl.semaphore_signal(
                barrier, inc=1, device_id=device(q, target_y, target_z, target_core), device_id_type=MESH
            )

        @pl.when(jnp.logical_not(diagonal & (z == q)))
        def _():
            pl.semaphore_signal(
                barrier, inc=1, device_id=device(from_x, from_y, q, from_core), device_id_type=MESH
            )
    find_weights(transitions, energies, occupations, frequencies, weight)
    pl.semaphore_wait(barrier, 15 - 2 * diagonal.astype(jnp.int32))

    sent = []

    def send(src, dst, sems, slot, there):
        copy = pltpu.make_async_remote_copy(
            src_ref=src, dst_ref=dst, send_sem=sems[0].at[slot], recv_sem=sems[1].at[slot],
            device_id=there, device_id_type=MESH,
        )
        copy.start()
        sent.append(copy)
        return copy

    rows, cols, both = (r_send, r_recv), (c_send, c_recv), (b_send, b_recv)

    def sibling(round_, slot, index):
        ref = colp.at[round_, :, slot]
        return send(ref, ref, both, index, to_sibling)

    own = pltpu.make_async_copy(pair, colp.at[0, :, mine], own_sem)
    own.start()
    c_part = send(pair, colp.at[0, :, mine], cols, 0, to_partner)
    shift = (z + 4 - target_z) % 4
    target_round = shift + (shift == 2).astype(jnp.int32) - (shift == 3).astype(jnp.int32)
    scatter = []
    for q in range(4):
        src = pair.at[:, pl.ds(16 * q, 16), :]
        dst = rowp.at[target_round, :, mine, q]
        remote = pltpu.make_async_remote_copy(
            src_ref=src, dst_ref=dst, send_sem=s_send.at[q], recv_sem=s_recv.at[target_round],
            device_id=device(q, target_y, target_z, target_core), device_id_type=MESH,
        )
        local = pltpu.make_async_copy(src, dst, s_recv.at[target_round])
        here = diagonal & (x == q)

        @pl.when(here)
        def _():
            local.start()

        @pl.when(jnp.logical_not(here))
        def _():
            remote.start()

        scatter.append((here, remote))
    c_zp = send(pair, colp.at[2, :, mine], cols, 1, to_zp)
    c_zm = send(pair, colp.at[1, :, mine], cols, 2, to_zm)
    s_own = send(pair, colp.at[0, :, mine], both, 0, to_sibling)
    waits = [s_own]
    needed = ((0, 1), (3, 4), (2, 5), (6, 7))

    gather = {}

    def step(stage, j):
        def ref(part, *index):
            return rowp.at[(j, part) + index]

        def go(name, ref, there):
            gather[j, name] = send(ref, ref, rows, 16 * j + name, there)

        def arrived(*names):
            for name in names:
                gather[j, name].wait_recv()
                gather[j, name + 1].wait_recv()

        if stage == 0:
            mine_ref = rowp.at[j, :, s0, x]
            pltpu.make_async_copy(mine_ref, mine_ref, s_recv.at[j]).wait()
            go(A1, ref(0, s0, x), to_xp)
            go(A1 + 1, ref(0, s0, x), to_xm)
            go(B1, ref(1, s0, x), to_partner)
            go(B1 + 1, ref(1, s0, x), to_next)
        if stage == 1:
            first, second = pl.ds(0, half), pl.ds(half, half)
            arrived(A1)
            go(A2, ref(0, s0, xm, slice(None), first), to_xp)
            go(A2 + 1, ref(0, s0, xp, slice(None), second), to_xm)
            arrived(B1)
            go(B2, ref(1, s_next, x, slice(None), first), to_partner)
            go(B2 + 1, ref(1, s_pair, x, slice(None), second), to_next)
        if stage == 2:
            arrived(A2)
            go(A3, ref(0, s0), to_partner)
            go(A3 + 1, ref(0, s0), to_next)
            arrived(B2)
            go(B3, ref(1, slice(None), x), to_xp)
            go(B3 + 1, ref(1, slice(None), x), to_xm)
        if stage == 3:
            arrived(A3)
            go(A4, ref(0, s_next, pl.ds(0, 1)), to_partner)
            go(A4 + 1, ref(0, s_pair, pl.ds(1, 3)), to_next)
            arrived(B3)
            go(B4, ref(1, pl.ds(0, 2), xm), to_xp)
            go(B4 + 1, ref(1, pl.ds(2, 2), xp), to_xm)
        if stage == 4:
            arrived(A4, B4)

    held = {}

    def col_event(n):
        if n == 0:
            c_part.wait_recv()
            ref = colp.at[0, :, partner]
            held["zp2"] = send(ref, colp.at[2, :, partner], cols, 3, to_zp)
            held["zm2"] = send(ref, colp.at[1, :, partner], cols, 4, to_zm)
            waits.append(sibling(0, partner, 1))
        if n == 1:
            c_zp.wait_recv()
            held["far"] = send(colp.at[2, :, mine], colp.at[3, :, mine], cols, 5, to_zp)
            waits.append(sibling(2, mine, 2))
            c_zm.wait_recv()
            waits.append(sibling(1, mine, 3))
        if n == 2:
            held["zm2"].wait_recv()
            held["far2"] = send(colp.at[1, :, partner], colp.at[3, :, partner], cols, 6, to_zm)
            waits.append(sibling(1, partner, 4))
            held["zp2"].wait_recv()
            waits.append(sibling(2, partner, 5))
        if n == 3:
            held["far"].wait_recv()
            waits.append(sibling(3, mine, 6))
            held["far2"].wait_recv()
            waits.append(sibling(3, partner, 7))

    for name, n in ORDER:
        if name == "c":
            col_event(n)
        elif name == "k":
            j = n // 2
            if n == 0:
                own.wait()
            if n % 2 == 0:
                for index in needed[j]:
                    waits[index].wait_recv()
            for tile in (n % 2 * 2, n % 2 * 2 + 1):
                for f, part, span, product in products(rowp, colp, weight, z, j, tile):
                    if j == 0:
                        total[f, part, span, :] = product
                    else:
                        total[f, part, span, :] += product
        else:
            step(name, n)
    for index in needed[3]:
        waits[index].wait_recv()
    for copy in sent:
        copy.wait_send()
    for here, remote in scatter:
        @pl.when(jnp.logical_not(here))
        def _():
            remote.wait_send()


def find_weights(transitions, energies, occupations, frequencies, weight):
    count = transitions.shape[1]
    bands, points = energies.shape
    kpoint, valence, conduction = transitions[0:1, :], transitions[1:2, :], transitions[2:3, :]
    pick = (lax.broadcasted_iota(jnp.int32, (points, count), 0) == kpoint).astype(jnp.float32)
    band = lax.broadcasted_iota(jnp.int32, (bands, count), 0)

    def of(table):
        values = jnp.dot(table, pick, precision=lax.Precision.HIGHEST, preferred_element_type=jnp.float32)

        def one(which):
            return jnp.sum(jnp.where(band == which, values, 0.0), axis=0, keepdims=True)

        return one(valence), one(conduction)

    low, high = of(energies[...])
    gap = high - low
    below, above = of(occupations[...].astype(jnp.float32))
    filled = below - above
    for f in range(weight.shape[0]):
        frequency = frequencies[f]
        weight[f : f + 1, :] = filled * 2.0 * gap / (gap * gap + frequency * frequency)


def products(rowp, colp, weight, z, j, tile):
    rows = pl.ds(TILE * tile, TILE)
    right = colp[j].reshape(-1, colp.shape[-1])
    depth = right.shape[0] // 2
    lefts = [rowp[j, part, :, :, :, rows].reshape(depth, TILE).T.astype(jnp.float32) for part in range(2)]
    start = pl.multiple_of(((z + SHIFT[j]) % 4) * depth, depth)
    for f in range(weight.shape[0]):
        w = weight[f : f + 1, pl.ds(start, depth)]
        first, second = [(left * w).astype(jnp.bfloat16) for left in lefts]
        for part, pair in enumerate(((first, second), (second, -first))):
            yield f, part, rows, jnp.dot(jnp.concatenate(pair, axis=1), right, preferred_element_type=jnp.float32)


def finish_kernel(rowp, colp, weight, total, out, stage, sems):
    z = where_am_i()[2]
    copies = []
    for tile in range(total.shape[2] // TILE):
        for f, part, rows, product in products(rowp, colp, weight, z, 3, tile):
            stage[f, part, rows, :] = total[f, part, rows, :] + product
            copy = pltpu.make_async_copy(
                stage.at[f, part, rows, :], out.at[f, part, rows, :], sems.at[tile, f, part]
            )
            copy.start()
            copies.append(copy)
    for copy in copies:
        copy.wait()


def body(pair_elements, transitions, energies, occupations, frequencies):
    width = pair_elements.shape[2]
    dma = pltpu.SemaphoreType.DMA
    vmem, smem = pl.BlockSpec(memory_space=pltpu.VMEM), pl.BlockSpec(memory_space=pltpu.SMEM)
    kept = pl.pallas_call(
        gather_kernel,
        out_shape=(
            pltpu.VMEM((4, 2, 4, 4, 16, width), jnp.bfloat16),
            pltpu.VMEM((4, 2, 4, 64, width), jnp.bfloat16),
            pltpu.VMEM((2, transitions.shape[1]), jnp.float32),
            pltpu.VMEM((2, 2, width, width), jnp.float32),
        ),
        in_specs=[vmem] * 4 + [smem],
        out_specs=[vmem] * 4,
        scratch_shapes=[
            dma, dma((4,)), dma((4,)), dma((64,)), dma((64,)), dma((7,)), dma((7,)), dma((8,)), dma((8,)),
        ],
        compiler_params=pltpu.CompilerParams(
            collective_id=0, has_side_effects=True, vmem_limit_bytes=8 * 2**20
        ),
    )(pair_elements, transitions, energies.T, occupations.T, frequencies)
    return pl.pallas_call(
        finish_kernel,
        out_shape=jax.ShapeDtypeStruct((2, 2, width, width), jnp.float32),
        in_specs=[vmem] * 4,
        out_specs=pl.BlockSpec(memory_space=pl.ANY),
        scratch_shapes=[pltpu.VMEM((2, 2, width, width), jnp.float32), dma((width // TILE, 2, 2))],
        compiler_params=pltpu.CompilerParams(vmem_limit_bytes=24 * 2**20),
    )(*kept)


def solution(mesh):
    in_specs = (P(None, ("row", "freq"), "col"), P(), P(), P(), P("freq"))
    out_specs = P("freq", None, "row", "col")
    return jax.shard_map(body, mesh=mesh, in_specs=in_specs, out_specs=out_specs, check_vma=False)
```

```python
import jax
import jax.numpy as jnp
from jax import lax
from jax.experimental import pallas as pl
from jax.experimental.pallas import tpu as pltpu
from jax.sharding import PartitionSpec as P

MESH = pl.DeviceIdType.MESH
ORDER = (
    "p0", "z0", "a00", "b00", "p1", "a01", "b01", "a10", "b10", "a02", "b02", "a11", "b11", "a20", "b20", "q0", "q1",
    "a03", "b03", "a12", "b12", "a21", "b21", "a30", "b30", "c1", "a13", "b13", "a22", "b22", "e0", "a31", "b31",
    "c2", "k0", "a23", "b23", "a32", "b32", "e1", "k1", "a33", "b33", "e2", "c3", "k2", "e3",
)

TILE = 256
SHIFT = (0, 1, 3, 2)
A1, A2, A3, A4, B1, B2, B3, B4 = range(0, 16, 2)


def where_am_i():
    row, col, low = lax.axis_index("row"), lax.axis_index("col"), lax.axis_index("freq")
    return col % 4, 2 * (col // 4) + low, row // 2, row % 2


def device(x, y, z, core):
    return (2 * (z % 4) + core, 4 * ((y % 4) // 2) + x % 4, y % 2)


def slot_of(y, z):
    delta = (y + 8 - 2 * (z // 2)) % 4
    return 2 * (delta // 2) + (delta + delta // 2) % 2


def gather_kernel(
    pair_hbm, transitions_hbm, energies_hbm, occupations_hbm, frequencies_hbm, rowp, colp, weight, total,
    pair, transitions, energies, occupations, frequencies, in_sem, own_sem, s_send, s_recv, r_send, r_recv,
    c_send, c_recv, b_send, b_recv,
):
    x, y, z, core = where_am_i()
    loads = [
        pltpu.make_async_copy(src, dst, in_sem.at[i])
        for i, (src, dst) in enumerate((
            (pair_hbm, pair), (transitions_hbm, transitions), (energies_hbm, energies),
            (occupations_hbm, occupations), (frequencies_hbm, frequencies),
        ))
    ]
    for load in loads:
        load.start()
    low = y % 2
    half = pair.shape[2] // 2
    diagonal = (2 * z + core == 4 * (y // 2) + x) & (core == 0)
    target_z, target_core = 2 * (y // 2) + x // 2, x % 2
    target_y = (y + 4 + core * (2 * low - 1)) % 4
    mine = 2 * core + low
    partner = 2 * core + 1 - low
    xm, xp = (x + 3) % 4, (x + 1) % 4
    y_pair, y_next = y + 1 - 2 * low, y + 3 + 2 * low
    s0, s_pair, s_next = slot_of(y, z), slot_of(y_pair, z), slot_of(y_next, z)
    to_partner, to_next = device(x, y_pair, z, core), device(x, y_next, z, core)
    to_xp, to_xm = device(x + 1, y, z, core), device(x + 3, y, z, core)
    to_zp, to_zm = device(x, y, z + 1, core), device(x, y, z + 3, core)
    to_sibling = device(x, y, z, 1 - core)

    delta = (y + 8 - 2 * (z // 2)) % 4
    from_core, from_low = delta // 2, (delta + delta // 2) % 2
    from_x, from_y = 2 * (z % 2) + core, 2 * (z // 2) + from_low

    barrier = pltpu.get_barrier_semaphore()
    for there in (to_xp, to_xm, to_partner, to_next, to_zp, to_zm, to_sibling):
        pl.semaphore_signal(barrier, inc=1, device_id=there, device_id_type=MESH)
    for q in range(4):
        @pl.when(jnp.logical_not(diagonal & (x == q)))
        def _():
            pl.semaphore_signal(
                barrier, inc=1, device_id=device(q, target_y, target_z, target_core), device_id_type=MESH
            )

        @pl.when(jnp.logical_not(diagonal & (z == q)))
        def _():
            pl.semaphore_signal(
                barrier, inc=1, device_id=device(from_x, from_y, q, from_core), device_id_type=MESH
            )
    for load in loads:
        load.wait()
    find_weights(transitions, energies, occupations, frequencies, weight)
    pl.semaphore_wait(barrier, 15 - 2 * diagonal.astype(jnp.int32))

    sent = []

    def send(src, dst, sems, slot, there):
        copy = pltpu.make_async_remote_copy(
            src_ref=src, dst_ref=dst, send_sem=sems[0].at[slot], recv_sem=sems[1].at[slot],
            device_id=there, device_id_type=MESH,
        )
        copy.start()
        sent.append(copy)
        return copy

    rows, cols, both = (r_send, r_recv), (c_send, c_recv), (b_send, b_recv)

    def sibling(round_, slot, index):
        ref = colp.at[round_, :, slot]
        return send(ref, ref, both, index, to_sibling)

    own = pltpu.make_async_copy(pair, colp.at[0, :, mine], own_sem)
    own.start()
    shift = (z + 4 - target_z) % 4
    target_round = shift + (shift == 2).astype(jnp.int32) - (shift == 3).astype(jnp.int32)
    scatter = []
    for q in range(4):
        src = pair.at[:, pl.ds(16 * q, 16), :]
        dst = rowp.at[target_round, :, mine, q]
        remote = pltpu.make_async_remote_copy(
            src_ref=src, dst_ref=dst, send_sem=s_send.at[q], recv_sem=s_recv.at[target_round],
            device_id=device(q, target_y, target_z, target_core), device_id_type=MESH,
        )
        local = pltpu.make_async_copy(src, dst, s_recv.at[target_round])
        here = diagonal & (x == q)

        @pl.when(here)
        def _():
            local.start()

        @pl.when(jnp.logical_not(here))
        def _():
            remote.start()

        scatter.append((here, remote))
    needed = ((0, 1), (3, 4), (2, 5), (6, 7))
    waits = {}
    held = {}

    gather = {}

    def step(stage, j):
        def ref(part, *index):
            return rowp.at[(j, part) + index]

        def go(name, ref, there):
            gather[j, name] = send(ref, ref, rows, 16 * j + name, there)

        def arrived(*names):
            for name in names:
                gather[j, name].wait_recv()
                gather[j, name + 1].wait_recv()

        first, second = pl.ds(0, half), pl.ds(half, half)
        if stage in ("a0", "b0") and ("s", j) not in held:
            held["s", j] = True
            mine_ref = rowp.at[j, :, s0, x]
            pltpu.make_async_copy(mine_ref, mine_ref, s_recv.at[j]).wait()
        if stage == "a0":
            go(A1, ref(0, s0, x), to_xp)
            go(A1 + 1, ref(0, s0, x), to_xm)
        if stage == "b0":
            go(B1, ref(1, s0, x), to_partner)
            go(B1 + 1, ref(1, s0, x), to_next)
        if stage == "a1":
            gather[j, A1].wait_recv()
            go(A2, ref(0, s0, xm, slice(None), first), to_xp)
            gather[j, A1 + 1].wait_recv()
            go(A2 + 1, ref(0, s0, xp, slice(None), second), to_xm)
        if stage == "b1":
            gather[j, B1 + 1].wait_recv()
            go(B2, ref(1, s_next, x, slice(None), first), to_partner)
            gather[j, B1].wait_recv()
            go(B2 + 1, ref(1, s_pair, x, slice(None), second), to_next)
        if stage == "a2":
            arrived(A2)
            go(A3, ref(0, s0), to_partner)
            go(A3 + 1, ref(0, s0), to_next)
        if stage == "b2":
            arrived(B2)
            go(B3, ref(1, slice(None), x), to_xp)
            go(B3 + 1, ref(1, slice(None), x), to_xm)
        if stage == "a3":
            gather[j, A3].wait_recv()
            go(A4 + 1, ref(0, s_pair, pl.ds(1, 3)), to_next)
            gather[j, A3 + 1].wait_recv()
            go(A4, ref(0, s_next, pl.ds(0, 1)), to_partner)
        if stage == "b3":
            gather[j, B3].wait_recv()
            go(B4, ref(1, pl.ds(0, 2), xm), to_xp)
            gather[j, B3 + 1].wait_recv()
            go(B4 + 1, ref(1, pl.ds(2, 2), xp), to_xm)
        if stage == "e":
            arrived(A4, B4)

    def col_event(name, n):
        if name == "p":
            held["p", n] = send(pair.at[n], colp.at[0, n, mine], cols, n, to_partner)
        if name == "z":
            held["zp"] = send(pair, colp.at[2, :, mine], cols, 2, to_zp)
            held["zm"] = send(pair, colp.at[1, :, mine], cols, 3, to_zm)
            waits[0] = send(pair, colp.at[0, :, mine], both, 0, to_sibling)
        if name == "q":
            held["p", n].wait_recv()
            ref = colp.at[0, n, partner]
            held["zp", n] = send(ref, colp.at[2, n, partner], cols, 4 + n, to_zp)
            held["zm", n] = send(ref, colp.at[1, n, partner], cols, 6 + n, to_zm)
            if n == 1:
                waits[1] = sibling(0, partner, 1)
        if name == "c" and n == 1:
            held["zp"].wait_recv()
            held["far"] = send(colp.at[2, :, mine], colp.at[3, :, mine], cols, 8, to_zp)
            waits[2] = sibling(2, mine, 2)
            held["zm"].wait_recv()
            waits[3] = sibling(1, mine, 3)
        if name == "c" and n == 2:
            for h in range(2):
                held["zm", h].wait_recv()
            held["far2"] = send(colp.at[1, :, partner], colp.at[3, :, partner], cols, 9, to_zm)
            waits[4] = sibling(1, partner, 4)
            for h in range(2):
                held["zp", h].wait_recv()
            waits[5] = sibling(2, partner, 5)
        if name == "c" and n == 3:
            held["far"].wait_recv()
            waits[6] = sibling(3, mine, 6)
            held["far2"].wait_recv()
            waits[7] = sibling(3, partner, 7)

    for word in ORDER:
        name, n = word[:-1], int(word[-1])
        if name in "pzqc":
            col_event(name, n)
        elif name == "k":
            if n == 0:
                own.wait()
            for index in needed[n]:
                waits[index].wait_recv()
            for tile in range(total.shape[2] // TILE):
                for f, part, span, product in products(rowp, colp, weight, z, n, tile):
                    if n == 0:
                        total[f, part, span, :] = product
                    else:
                        total[f, part, span, :] += product
        else:
            step(name, n)
    for index in needed[3]:
        waits[index].wait_recv()
    for copy in sent:
        copy.wait_send()
    for here, remote in scatter:
        @pl.when(jnp.logical_not(here))
        def _():
            remote.wait_send()


def find_weights(transitions, energies, occupations, frequencies, weight):
    count = transitions.shape[1]
    points, bands = energies.shape
    kpoint, valence, conduction = transitions[0:1, :], transitions[1:2, :], transitions[2:3, :]
    pick = (lax.broadcasted_iota(jnp.int32, (points, count), 0) == kpoint).astype(jnp.float32)
    band = lax.broadcasted_iota(jnp.int32, (bands, count), 0)

    def of(table):
        values = lax.dot_general(
            table, pick, (((0,), (0,)), ((), ())), precision=lax.Precision.HIGHEST, preferred_element_type=jnp.float32
        )

        def one(which):
            return jnp.sum(jnp.where(band == which, values, 0.0), axis=0, keepdims=True)

        return one(valence), one(conduction)

    low, high = of(energies[...])
    gap = high - low
    below, above = of(occupations[...].astype(jnp.float32))
    filled = below - above
    for f in range(weight.shape[0]):
        frequency = frequencies[f]
        weight[f : f + 1, :] = filled * 2.0 * gap / (gap * gap + frequency * frequency)


def products(rowp, colp, weight, z, j, tile):
    rows = pl.ds(TILE * tile, TILE)
    right = colp[j].reshape(-1, colp.shape[-1])
    depth = right.shape[0] // 2
    lefts = [rowp[j, part, :, :, :, rows].reshape(depth, TILE).T.astype(jnp.float32) for part in range(2)]
    start = pl.multiple_of(((z + SHIFT[j]) % 4) * depth, depth)
    for f in range(weight.shape[0]):
        w = weight[f : f + 1, pl.ds(start, depth)]
        first, second = [(left * w).astype(jnp.bfloat16) for left in lefts]
        for part, pair in enumerate(((first, second), (second, -first))):
            yield f, part, rows, jnp.dot(jnp.concatenate(pair, axis=1), right, preferred_element_type=jnp.float32)


def finish_kernel(rowp, colp, weight, total, out, stage, sems):
    z = where_am_i()[2]
    copies = []
    for tile in range(total.shape[2] // TILE):
        for f, part, rows, product in products(rowp, colp, weight, z, 3, tile):
            stage[f, part, rows, :] = total[f, part, rows, :] + product
            copy = pltpu.make_async_copy(
                stage.at[f, part, rows, :], out.at[f, part, rows, :], sems.at[tile, f, part]
            )
            copy.start()
            copies.append(copy)
    for copy in copies:
        copy.wait()


def body(pair_elements, transitions, energies, occupations, frequencies):
    width = pair_elements.shape[2]
    dma = pltpu.SemaphoreType.DMA
    vmem = pl.BlockSpec(memory_space=pltpu.VMEM)
    inputs = [
        pltpu.with_memory_space_constraint(value, pltpu.HBM)
        for value in (pair_elements, transitions, energies, occupations, frequencies)
    ]
    kept = pl.pallas_call(
        gather_kernel,
        out_shape=(
            pltpu.VMEM((4, 2, 4, 4, 16, width), jnp.bfloat16),
            pltpu.VMEM((4, 2, 4, 64, width), jnp.bfloat16),
            pltpu.VMEM((2, transitions.shape[1]), jnp.float32),
            pltpu.VMEM((2, 2, width, width), jnp.float32),
        ),
        in_specs=[pl.BlockSpec(memory_space=pltpu.HBM)] * 5,
        out_specs=[vmem] * 4,
        scratch_shapes=[
            pltpu.VMEM(pair_elements.shape, jnp.bfloat16),
            pltpu.VMEM(transitions.shape, jnp.int32),
            pltpu.VMEM(energies.shape, jnp.float32),
            pltpu.VMEM(occupations.shape, jnp.int32),
            pltpu.SMEM(frequencies.shape, jnp.float32),
            dma((5,)), dma, dma((4,)), dma((4,)), dma((64,)), dma((64,)), dma((10,)), dma((10,)), dma((8,)), dma((8,)),
        ],
        compiler_params=pltpu.CompilerParams(
            collective_id=0, has_side_effects=True, vmem_limit_bytes=8 * 2**20
        ),
    )(*inputs)
    return pl.pallas_call(
        finish_kernel,
        out_shape=jax.ShapeDtypeStruct((2, 2, width, width), jnp.float32),
        in_specs=[vmem] * 4,
        out_specs=pl.BlockSpec(memory_space=pl.ANY),
        scratch_shapes=[pltpu.VMEM((2, 2, width, width), jnp.float32), dma((width // TILE, 2, 2))],
        compiler_params=pltpu.CompilerParams(vmem_limit_bytes=24 * 2**20),
    )(*kept)


def solution(mesh):
    in_specs = (P(None, ("row", "freq"), "col"), P(), P(), P(), P("freq"))
    out_specs = P("freq", None, "row", "col")
    return jax.shard_map(body, mesh=mesh, in_specs=in_specs, out_specs=out_specs, check_vma=False)
```

```python
import jax
import jax.numpy as jnp
from jax import lax
from jax.experimental import pallas as pl
from jax.experimental.pallas import tpu as pltpu
from jax.sharding import PartitionSpec as P

MESH = pl.DeviceIdType.MESH
ORDER = (
    "p0", "z0", "a00", "b00", "p1", "a01", "b01", "a10", "b10", "a02", "b02", "a11", "b11", "a20", "b20", "q0", "q1",
    "a03", "b03", "a12", "b12", "a21", "b21", "a30", "b30", "c1", "a13", "b13", "a22", "b22", "e0", "a31", "b31",
    "c2", "k0", "a23", "b23", "a32", "b32", "e1", "k1", "a33", "b33", "e2", "c3", "k2", "e3",
)

TILE = 256
SHIFT = (0, 1, 3, 2)
A1, A2, A3, A4, B1, B2, B3, B4 = range(0, 16, 2)


def where_am_i():
    row, col, low = lax.axis_index("row"), lax.axis_index("col"), lax.axis_index("freq")
    return col % 4, 2 * (col // 4) + low, row // 2, row % 2


def device(x, y, z, core):
    return (2 * (z % 4) + core, 4 * ((y % 4) // 2) + x % 4, y % 2)


def slot_of(y, z):
    delta = (y + 8 - 2 * (z // 2)) % 4
    return 2 * (delta // 2) + (delta + delta // 2) % 2


def gather_kernel(
    pair_hbm, transitions_hbm, energies_hbm, occupations_hbm, frequencies_hbm, rowp, colp, weight, total,
    pair, transitions, energies, occupations, frequencies, in_sem, own_sem, s_send, s_recv, r_send, r_recv,
    c_send, c_recv, b_send, b_recv,
):
    x, y, z, core = where_am_i()
    loads = [
        pltpu.make_async_copy(src, dst, in_sem.at[i])
        for i, (src, dst) in enumerate((
            (pair_hbm, pair), (transitions_hbm, transitions), (energies_hbm, energies),
            (occupations_hbm, occupations), (frequencies_hbm, frequencies),
        ))
    ]
    for load in loads:
        load.start()
    low = y % 2
    half = pair.shape[2] // 2
    diagonal = (2 * z + core == 4 * (y // 2) + x) & (core == 0)
    target_z, target_core = 2 * (y // 2) + x // 2, x % 2
    target_y = (y + 4 + core * (2 * low - 1)) % 4
    mine = 2 * core + low
    partner = 2 * core + 1 - low
    xm, xp = (x + 3) % 4, (x + 1) % 4
    y_pair, y_next = y + 1 - 2 * low, y + 3 + 2 * low
    s0, s_pair, s_next = slot_of(y, z), slot_of(y_pair, z), slot_of(y_next, z)
    to_partner, to_next = device(x, y_pair, z, core), device(x, y_next, z, core)
    to_xp, to_xm = device(x + 1, y, z, core), device(x + 3, y, z, core)
    to_zp, to_zm = device(x, y, z + 1, core), device(x, y, z + 3, core)
    to_sibling = device(x, y, z, 1 - core)

    delta = (y + 8 - 2 * (z // 2)) % 4
    from_core, from_low = delta // 2, (delta + delta // 2) % 2
    from_x, from_y = 2 * (z % 2) + core, 2 * (z // 2) + from_low

    barrier = pltpu.get_barrier_semaphore()
    for there in (to_xp, to_xm, to_partner, to_next, to_zp, to_zm, to_sibling):
        pl.semaphore_signal(barrier, inc=1, device_id=there, device_id_type=MESH)
    for q in range(4):
        @pl.when(jnp.logical_not(diagonal & (x == q)))
        def _():
            pl.semaphore_signal(
                barrier, inc=1, device_id=device(q, target_y, target_z, target_core), device_id_type=MESH
            )

        @pl.when(jnp.logical_not(diagonal & (z == q)))
        def _():
            pl.semaphore_signal(
                barrier, inc=1, device_id=device(from_x, from_y, q, from_core), device_id_type=MESH
            )
    for load in loads:
        load.wait()
    find_weights(transitions, energies, occupations, frequencies, weight)
    pl.semaphore_wait(barrier, 15 - 2 * diagonal.astype(jnp.int32))

    sent = []

    def send(src, dst, sems, slot, there):
        shared = sems[0] is r_send
        copy = pltpu.make_async_remote_copy(
            src_ref=src, dst_ref=dst, send_sem=sems[0].at[slot // 16 if shared else slot], recv_sem=sems[1].at[slot],
            device_id=there, device_id_type=MESH,
        )
        copy.start()
        if not shared:
            sent.append(copy)
        return copy

    rows, cols, both = (r_send, r_recv), (c_send, c_recv), (b_send, b_recv)

    def sibling(round_, slot, index):
        ref = colp.at[round_, :, slot]
        return send(ref, ref, both, index, to_sibling)

    own = pltpu.make_async_copy(pair, colp.at[0, :, mine], own_sem)
    own.start()
    shift = (z + 4 - target_z) % 4
    target_round = shift + (shift == 2).astype(jnp.int32) - (shift == 3).astype(jnp.int32)
    scatter = []
    for q in range(4):
        src = pair.at[:, pl.ds(16 * q, 16), :]
        dst = rowp.at[target_round, :, mine, q]
        remote = pltpu.make_async_remote_copy(
            src_ref=src, dst_ref=dst, send_sem=s_send.at[q], recv_sem=s_recv.at[target_round],
            device_id=device(q, target_y, target_z, target_core), device_id_type=MESH,
        )
        local = pltpu.make_async_copy(src, dst, s_recv.at[target_round])
        here = diagonal & (x == q)

        @pl.when(here)
        def _():
            local.start()

        @pl.when(jnp.logical_not(here))
        def _():
            remote.start()

        scatter.append((here, remote))
    needed = ((0, 1), (3, 4), (2, 5), (6, 7))
    waits = {}
    held = {}

    gather = {}

    def step(stage, j):
        def ref(part, *index):
            return rowp.at[(j, part) + index]

        def go(name, ref, there):
            gather[j, name] = send(ref, ref, rows, 16 * j + name, there)

        def arrived(*names):
            for name in names:
                gather[j, name].wait_recv()
                gather[j, name + 1].wait_recv()

        first, second = pl.ds(0, half), pl.ds(half, half)
        if stage in ("a0", "b0") and ("s", j) not in held:
            held["s", j] = True
            mine_ref = rowp.at[j, :, s0, x]
            pltpu.make_async_copy(mine_ref, mine_ref, s_recv.at[j]).wait()
        if stage == "a0":
            go(A1, ref(0, s0, x), to_xp)
            go(A1 + 1, ref(0, s0, x), to_xm)
        if stage == "b0":
            go(B1, ref(1, s0, x), to_partner)
            go(B1 + 1, ref(1, s0, x), to_next)
        if stage == "a1":
            gather[j, A1].wait_recv()
            go(A2, ref(0, s0, xm, slice(None), first), to_xp)
            gather[j, A1 + 1].wait_recv()
            go(A2 + 1, ref(0, s0, xp, slice(None), second), to_xm)
        if stage == "b1":
            gather[j, B1 + 1].wait_recv()
            go(B2, ref(1, s_next, x, slice(None), first), to_partner)
            gather[j, B1].wait_recv()
            go(B2 + 1, ref(1, s_pair, x, slice(None), second), to_next)
        if stage == "a2":
            arrived(A2)
            go(A3, ref(0, s0), to_partner)
            go(A3 + 1, ref(0, s0), to_next)
        if stage == "b2":
            arrived(B2)
            go(B3, ref(1, slice(None), x), to_xp)
            go(B3 + 1, ref(1, slice(None), x), to_xm)
        if stage == "a3":
            gather[j, A3].wait_recv()
            go(A4 + 1, ref(0, s_pair, pl.ds(2, 2)), to_next)
            gather[j, A3 + 1].wait_recv()
            go(A4, ref(0, s_next, pl.ds(0, 2)), to_partner)
        if stage == "b3":
            gather[j, B3].wait_recv()
            go(B4, ref(1, pl.ds(0, 2), xm), to_xp)
            gather[j, B3 + 1].wait_recv()
            go(B4 + 1, ref(1, pl.ds(2, 2), xp), to_xm)
        if stage == "e":
            arrived(A4, B4)

    def col_event(name, n):
        if name == "p":
            held["p", n] = send(pair.at[n], colp.at[0, n, mine], cols, n, to_partner)
        if name == "z":
            held["zp"] = send(pair, colp.at[2, :, mine], cols, 2, to_zp)
            held["zm"] = send(pair, colp.at[1, :, mine], cols, 3, to_zm)
            waits[0] = send(pair, colp.at[0, :, mine], both, 0, to_sibling)
        if name == "q":
            held["p", n].wait_recv()
            ref = colp.at[0, n, partner]
            held["zp", n] = send(ref, colp.at[2, n, partner], cols, 4 + n, to_zp)
            held["zm", n] = send(ref, colp.at[1, n, partner], cols, 6 + n, to_zm)
            if n == 1:
                waits[1] = sibling(0, partner, 1)
        if name == "c" and n == 1:
            held["zp"].wait_recv()
            held["far"] = send(colp.at[2, :, mine], colp.at[3, :, mine], cols, 8, to_zp)
            waits[2] = sibling(2, mine, 2)
            held["zm"].wait_recv()
            waits[3] = sibling(1, mine, 3)
        if name == "c" and n == 2:
            for h in range(2):
                held["zm", h].wait_recv()
            held["far2"] = send(colp.at[1, :, partner], colp.at[3, :, partner], cols, 9, to_zm)
            waits[4] = sibling(1, partner, 4)
            for h in range(2):
                held["zp", h].wait_recv()
            waits[5] = sibling(2, partner, 5)
        if name == "c" and n == 3:
            held["far"].wait_recv()
            waits[6] = sibling(3, mine, 6)
            held["far2"].wait_recv()
            waits[7] = sibling(3, partner, 7)

    for word in ORDER:
        name, n = word[:-1], int(word[-1])
        if name in "pzqc":
            col_event(name, n)
        elif name == "k":
            if n == 0:
                own.wait()
            for index in needed[n]:
                waits[index].wait_recv()
            for tile in range(total.shape[2] // TILE):
                for f, part, span, product in products(rowp, colp, weight, z, n, tile):
                    if n == 0:
                        total[f, part, span, :] = product
                    else:
                        total[f, part, span, :] += product
        else:
            step(name, n)
    for index in needed[3]:
        waits[index].wait_recv()
    for copy in sent:
        copy.wait_send()
    for j in range(4):
        rows_sent = total.at[0, 0, pl.ds(0, 240), :]
        pltpu.make_async_remote_copy(
            src_ref=rows_sent, dst_ref=rows_sent, send_sem=r_send.at[j], recv_sem=r_recv.at[0],
            device_id=to_sibling, device_id_type=MESH,
        ).wait_send()
    for here, remote in scatter:
        @pl.when(jnp.logical_not(here))
        def _():
            remote.wait_send()


def find_weights(transitions, energies, occupations, frequencies, weight):
    count = transitions.shape[1]
    points, bands = energies.shape
    kpoint, valence, conduction = transitions[0:1, :], transitions[1:2, :], transitions[2:3, :]
    pick = (lax.broadcasted_iota(jnp.int32, (points, count), 0) == kpoint).astype(jnp.float32)
    band = lax.broadcasted_iota(jnp.int32, (bands, count), 0)

    def of(table):
        values = lax.dot_general(
            table, pick, (((0,), (0,)), ((), ())), precision=lax.Precision.HIGHEST, preferred_element_type=jnp.float32
        )

        def one(which):
            return jnp.sum(jnp.where(band == which, values, 0.0), axis=0, keepdims=True)

        return one(valence), one(conduction)

    low, high = of(energies[...])
    gap = high - low
    below, above = of(occupations[...].astype(jnp.float32))
    filled = below - above
    for f in range(weight.shape[0]):
        frequency = frequencies[f]
        weight[f : f + 1, :] = filled * 2.0 * gap / (gap * gap + frequency * frequency)


def products(rowp, colp, weight, z, j, tile):
    rows = pl.ds(TILE * tile, TILE)
    right = colp[j].reshape(-1, colp.shape[-1])
    depth = right.shape[0] // 2
    lefts = [rowp[j, part, :, :, :, rows].reshape(depth, TILE).T.astype(jnp.float32) for part in range(2)]
    start = pl.multiple_of(((z + SHIFT[j]) % 4) * depth, depth)
    for f in range(weight.shape[0]):
        w = weight[f : f + 1, pl.ds(start, depth)]
        first, second = [(left * w).astype(jnp.bfloat16) for left in lefts]
        for part, pair in enumerate(((first, second), (second, -first))):
            yield f, part, rows, jnp.dot(jnp.concatenate(pair, axis=1), right, preferred_element_type=jnp.float32)


def finish_kernel(rowp, colp, weight, total, out, stage, sems):
    z = where_am_i()[2]
    copies = []
    for tile in range(total.shape[2] // TILE):
        for f, part, rows, product in products(rowp, colp, weight, z, 3, tile):
            stage[f, part, rows, :] = total[f, part, rows, :] + product
            copy = pltpu.make_async_copy(
                stage.at[f, part, rows, :], out.at[f, part, rows, :], sems.at[tile, f, part]
            )
            copy.start()
            copies.append(copy)
    for copy in copies:
        copy.wait()


def body(pair_elements, transitions, energies, occupations, frequencies):
    width = pair_elements.shape[2]
    dma = pltpu.SemaphoreType.DMA
    vmem = pl.BlockSpec(memory_space=pltpu.VMEM)
    inputs = [
        pltpu.with_memory_space_constraint(value, pltpu.HBM)
        for value in (pair_elements, transitions, energies, occupations, frequencies)
    ]
    kept = pl.pallas_call(
        gather_kernel,
        out_shape=(
            pltpu.VMEM((4, 2, 4, 4, 16, width), jnp.bfloat16),
            pltpu.VMEM((4, 2, 4, 64, width), jnp.bfloat16),
            pltpu.VMEM((2, transitions.shape[1]), jnp.float32),
            pltpu.VMEM((2, 2, width, width), jnp.float32),
        ),
        in_specs=[pl.BlockSpec(memory_space=pltpu.HBM)] * 5,
        out_specs=[vmem] * 4,
        scratch_shapes=[
            pltpu.VMEM(pair_elements.shape, jnp.bfloat16),
            pltpu.VMEM(transitions.shape, jnp.int32),
            pltpu.VMEM(energies.shape, jnp.float32),
            pltpu.VMEM(occupations.shape, jnp.int32),
            pltpu.SMEM(frequencies.shape, jnp.float32),
            dma((5,)), dma, dma((4,)), dma((4,)), dma((4,)), dma((64,)), dma((10,)), dma((10,)), dma((8,)), dma((8,)),
        ],
        compiler_params=pltpu.CompilerParams(
            collective_id=0, has_side_effects=True, vmem_limit_bytes=8 * 2**20
        ),
    )(*inputs)
    return pl.pallas_call(
        finish_kernel,
        out_shape=jax.ShapeDtypeStruct((2, 2, width, width), jnp.float32),
        in_specs=[vmem] * 4,
        out_specs=pl.BlockSpec(memory_space=pl.ANY),
        scratch_shapes=[pltpu.VMEM((2, 2, width, width), jnp.float32), dma((width // TILE, 2, 2))],
        compiler_params=pltpu.CompilerParams(vmem_limit_bytes=24 * 2**20),
    )(*kept)


def solution(mesh):
    in_specs = (P(None, ("row", "freq"), "col"), P(), P(), P(), P("freq"))
    out_specs = P("freq", None, "row", "col")
    return jax.shard_map(body, mesh=mesh, in_specs=in_specs, out_specs=out_specs, check_vma=False)
```

```python
import jax
import jax.numpy as jnp
from jax import lax
from jax.experimental import pallas as pl
from jax.experimental.pallas import tpu as pltpu
from jax.sharding import PartitionSpec as P

MESH = pl.DeviceIdType.MESH
ORDER = (
    "p0", "z0", "a00", "b00", "p1", "a01", "b01", "a10", "b10", "a02", "b02", "a11", "b11", "a20", "b20", "q0", "q1",
    "a03", "b03", "a12", "b12", "a21", "b21", "a30", "b30", "c1", "a13", "b13", "a22", "b22", "e0", "a31", "b31",
    "c2", "a23", "b23", "k0", "a32", "b32", "e1", "k1", "a33", "b33", "e2", "c3", "k2", "e3",
)

TILE = 256
SHIFT = (0, 1, 3, 2)
A1, A2, A3, A4, B1, B2, B3, B4 = range(0, 16, 2)


def where_am_i():
    row, col, low = lax.axis_index("row"), lax.axis_index("col"), lax.axis_index("freq")
    return col % 4, 2 * (col // 4) + low, row // 2, row % 2


def device(x, y, z, core):
    return (2 * (z % 4) + core, 4 * ((y % 4) // 2) + x % 4, y % 2)


def slot_of(y, z):
    delta = (y + 8 - 2 * (z // 2)) % 4
    return 2 * (delta // 2) + (delta + delta // 2) % 2


def gather_kernel(
    pair_hbm, transitions_hbm, energies_hbm, occupations_hbm, frequencies_hbm, rowp, colp, weight, total,
    pair, transitions, energies, occupations, frequencies, in_sem, own_sem, s_send, s_recv, r_send, r_recv,
    c_send, c_recv, b_send, b_recv,
):
    x, y, z, core = where_am_i()
    loads = [
        pltpu.make_async_copy(src, dst, in_sem.at[i])
        for i, (src, dst) in enumerate((
            (pair_hbm, pair), (transitions_hbm, transitions), (energies_hbm, energies),
            (occupations_hbm, occupations), (frequencies_hbm, frequencies),
        ))
    ]
    for load in loads:
        load.start()
    low = y % 2
    half = pair.shape[2] // 2
    diagonal = (2 * z + core == 4 * (y // 2) + x) & (core == 0)
    target_z, target_core = 2 * (y // 2) + x // 2, x % 2
    target_y = (y + 4 + core * (2 * low - 1)) % 4
    mine = 2 * core + low
    partner = 2 * core + 1 - low
    xm, xp = (x + 3) % 4, (x + 1) % 4
    y_pair, y_next = y + 1 - 2 * low, y + 3 + 2 * low
    s0, s_pair, s_next = slot_of(y, z), slot_of(y_pair, z), slot_of(y_next, z)
    to_partner, to_next = device(x, y_pair, z, core), device(x, y_next, z, core)
    to_xp, to_xm = device(x + 1, y, z, core), device(x + 3, y, z, core)
    to_zp, to_zm = device(x, y, z + 1, core), device(x, y, z + 3, core)
    to_sibling = device(x, y, z, 1 - core)

    delta = (y + 8 - 2 * (z // 2)) % 4
    from_core, from_low = delta // 2, (delta + delta // 2) % 2
    from_x, from_y = 2 * (z % 2) + core, 2 * (z // 2) + from_low

    barrier = pltpu.get_barrier_semaphore()
    for there in (to_xp, to_xm, to_partner, to_next, to_zp, to_zm, to_sibling):
        pl.semaphore_signal(barrier, inc=1, device_id=there, device_id_type=MESH)
    for q in range(4):
        @pl.when(jnp.logical_not(diagonal & (x == q)))
        def _():
            pl.semaphore_signal(
                barrier, inc=1, device_id=device(q, target_y, target_z, target_core), device_id_type=MESH
            )

        @pl.when(jnp.logical_not(diagonal & (z == q)))
        def _():
            pl.semaphore_signal(
                barrier, inc=1, device_id=device(from_x, from_y, q, from_core), device_id_type=MESH
            )
    for load in loads:
        load.wait()
    find_weights(transitions, energies, occupations, frequencies, weight)
    pl.semaphore_wait(barrier, 15 - 2 * diagonal.astype(jnp.int32))

    sent = []

    def send(src, dst, sems, slot, there):
        shared = sems[0] is r_send
        copy = pltpu.make_async_remote_copy(
            src_ref=src, dst_ref=dst, send_sem=sems[0].at[slot // 16 if shared else slot], recv_sem=sems[1].at[slot],
            device_id=there, device_id_type=MESH,
        )
        copy.start()
        if not shared:
            sent.append(copy)
        return copy

    rows, cols, both = (r_send, r_recv), (c_send, c_recv), (b_send, b_recv)

    def sibling(round_, slot, index):
        ref = colp.at[round_, :, slot]
        return send(ref, ref, both, index, to_sibling)

    own = pltpu.make_async_copy(pair, colp.at[0, :, mine], own_sem)
    own.start()
    shift = (z + 4 - target_z) % 4
    target_round = shift + (shift == 2).astype(jnp.int32) - (shift == 3).astype(jnp.int32)
    scatter = []
    for q in range(4):
        src = pair.at[:, pl.ds(16 * q, 16), :]
        dst = rowp.at[target_round, :, mine, q]
        remote = pltpu.make_async_remote_copy(
            src_ref=src, dst_ref=dst, send_sem=s_send.at[q], recv_sem=s_recv.at[target_round],
            device_id=device(q, target_y, target_z, target_core), device_id_type=MESH,
        )
        local = pltpu.make_async_copy(src, dst, s_recv.at[target_round])
        here = diagonal & (x == q)

        @pl.when(here)
        def _():
            local.start()

        @pl.when(jnp.logical_not(here))
        def _():
            remote.start()

        scatter.append((here, remote))
    needed = ((0, 1), (3, 4), (2, 5), (6, 7))
    waits = {}
    held = {}

    gather = {}

    def step(stage, j):
        def ref(part, *index):
            return rowp.at[(j, part) + index]

        def go(name, ref, there):
            gather[j, name] = send(ref, ref, rows, 16 * j + name, there)

        def arrived(*names):
            for name in names:
                gather[j, name].wait_recv()
                gather[j, name + 1].wait_recv()

        first, second = pl.ds(0, half), pl.ds(half, half)
        if stage in ("a0", "b0") and ("s", j) not in held:
            held["s", j] = True
            mine_ref = rowp.at[j, :, s0, x]
            pltpu.make_async_copy(mine_ref, mine_ref, s_recv.at[j]).wait()
        if stage == "a0":
            go(A1, ref(0, s0, x), to_xp)
            go(A1 + 1, ref(0, s0, x), to_xm)
        if stage == "b0":
            go(B1, ref(1, s0, x), to_partner)
            go(B1 + 1, ref(1, s0, x), to_next)
        if stage == "a1":
            gather[j, A1].wait_recv()
            go(A2, ref(0, s0, xm, slice(None), first), to_xp)
            gather[j, A1 + 1].wait_recv()
            go(A2 + 1, ref(0, s0, xp, slice(None), second), to_xm)
        if stage == "b1":
            gather[j, B1 + 1].wait_recv()
            go(B2, ref(1, s_next, x, slice(None), first), to_partner)
            gather[j, B1].wait_recv()
            go(B2 + 1, ref(1, s_pair, x, slice(None), second), to_next)
        if stage == "a2":
            arrived(A2)
            go(A3, ref(0, s0), to_partner)
            go(A3 + 1, ref(0, s0), to_next)
        if stage == "b2":
            arrived(B2)
            go(B3, ref(1, slice(None), x), to_xp)
            go(B3 + 1, ref(1, slice(None), x), to_xm)
        if stage == "a3":
            gather[j, A3].wait_recv()
            go(A4 + 1, ref(0, s_pair, pl.ds(2, 2)), to_next)
            gather[j, A3 + 1].wait_recv()
            go(A4, ref(0, s_next, pl.ds(0, 2)), to_partner)
        if stage == "b3":
            gather[j, B3].wait_recv()
            go(B4, ref(1, pl.ds(0, 2), xm), to_xp)
            gather[j, B3 + 1].wait_recv()
            go(B4 + 1, ref(1, pl.ds(2, 2), xp), to_xm)
        if stage == "e":
            arrived(A4, B4)

    def col_event(name, n):
        if name == "p":
            held["p", n] = send(pair.at[n], colp.at[0, n, mine], cols, n, to_partner)
        if name == "z":
            held["zp"] = send(pair, colp.at[2, :, mine], cols, 2, to_zp)
            held["zm"] = send(pair, colp.at[1, :, mine], cols, 3, to_zm)
            waits[0] = send(pair, colp.at[0, :, mine], both, 0, to_sibling)
        if name == "q":
            held["p", n].wait_recv()
            ref = colp.at[0, n, partner]
            held["zp", n] = send(ref, colp.at[2, n, partner], cols, 4 + n, to_zp)
            held["zm", n] = send(ref, colp.at[1, n, partner], cols, 6 + n, to_zm)
            if n == 1:
                waits[1] = sibling(0, partner, 1)
        if name == "c" and n == 1:
            held["zp"].wait_recv()
            held["far"] = send(colp.at[2, :, mine], colp.at[3, :, mine], cols, 8, to_zp)
            waits[2] = sibling(2, mine, 2)
            held["zm"].wait_recv()
            waits[3] = sibling(1, mine, 3)
        if name == "c" and n == 2:
            for h in range(2):
                held["zm", h].wait_recv()
            held["far2"] = send(colp.at[1, :, partner], colp.at[3, :, partner], cols, 9, to_zm)
            waits[4] = sibling(1, partner, 4)
            for h in range(2):
                held["zp", h].wait_recv()
            waits[5] = sibling(2, partner, 5)
        if name == "c" and n == 3:
            held["far"].wait_recv()
            waits[6] = sibling(3, mine, 6)
            held["far2"].wait_recv()
            waits[7] = sibling(3, partner, 7)

    for word in ORDER:
        name, n = word[:-1], int(word[-1])
        if name in "pzqc":
            col_event(name, n)
        elif name == "k":
            if n == 0:
                own.wait()
            for index in needed[n]:
                waits[index].wait_recv()
            for tile in range(total.shape[2] // TILE):
                for f, part, span, product in products(rowp, colp, weight, z, n, tile):
                    if n == 0:
                        total[f, part, span, :] = product
                    else:
                        total[f, part, span, :] += product
        else:
            step(name, n)
    for index in needed[3]:
        waits[index].wait_recv()
    for copy in sent:
        copy.wait_send()
    for j in range(4):
        rows_sent = total.at[0, 0, pl.ds(0, 240), :]
        pltpu.make_async_remote_copy(
            src_ref=rows_sent, dst_ref=rows_sent, send_sem=r_send.at[j], recv_sem=r_recv.at[0],
            device_id=to_sibling, device_id_type=MESH,
        ).wait_send()
    for here, remote in scatter:
        @pl.when(jnp.logical_not(here))
        def _():
            remote.wait_send()


def find_weights(transitions, energies, occupations, frequencies, weight):
    count = transitions.shape[1]
    points, bands = energies.shape
    kpoint, valence, conduction = transitions[0:1, :], transitions[1:2, :], transitions[2:3, :]
    pick = (lax.broadcasted_iota(jnp.int32, (points, count), 0) == kpoint).astype(jnp.float32)
    band = lax.broadcasted_iota(jnp.int32, (bands, count), 0)

    def of(table):
        values = lax.dot_general(
            table, pick, (((0,), (0,)), ((), ())), precision=lax.Precision.HIGHEST, preferred_element_type=jnp.float32
        )

        def one(which):
            return jnp.sum(jnp.where(band == which, values, 0.0), axis=0, keepdims=True)

        return one(valence), one(conduction)

    low, high = of(energies[...])
    gap = high - low
    below, above = of(occupations[...].astype(jnp.float32))
    filled = below - above
    for f in range(weight.shape[0]):
        frequency = frequencies[f]
        weight[f : f + 1, :] = filled * 2.0 * gap / (gap * gap + frequency * frequency)


def products(rowp, colp, weight, z, j, tile):
    rows = pl.ds(TILE * tile, TILE)
    right = colp[j].reshape(-1, colp.shape[-1])
    depth = right.shape[0] // 2
    lefts = [rowp[j, part, :, :, :, rows].reshape(depth, TILE).T.astype(jnp.float32) for part in range(2)]
    start = pl.multiple_of(((z + SHIFT[j]) % 4) * depth, depth)
    for f in range(weight.shape[0]):
        w = weight[f : f + 1, pl.ds(start, depth)]
        first, second = [(left * w).astype(jnp.bfloat16) for left in lefts]
        for part, pair in enumerate(((first, second), (second, -first))):
            yield f, part, rows, jnp.dot(jnp.concatenate(pair, axis=1), right, preferred_element_type=jnp.float32)


def finish_kernel(rowp, colp, weight, total, out, stage, sems):
    z = where_am_i()[2]
    copies = []
    for tile in range(total.shape[2] // TILE):
        for f, part, rows, product in products(rowp, colp, weight, z, 3, tile):
            stage[f, part, rows, :] = total[f, part, rows, :] + product
            copy = pltpu.make_async_copy(
                stage.at[f, part, rows, :], out.at[f, part, rows, :], sems.at[tile, f, part]
            )
            copy.start()
            copies.append(copy)
    for copy in copies:
        copy.wait()


def body(pair_elements, transitions, energies, occupations, frequencies):
    width = pair_elements.shape[2]
    dma = pltpu.SemaphoreType.DMA
    vmem = pl.BlockSpec(memory_space=pltpu.VMEM)
    inputs = [
        pltpu.with_memory_space_constraint(value, pltpu.HBM)
        for value in (pair_elements, transitions, energies, occupations, frequencies)
    ]
    kept = pl.pallas_call(
        gather_kernel,
        out_shape=(
            pltpu.VMEM((4, 2, 4, 4, 16, width), jnp.bfloat16),
            pltpu.VMEM((4, 2, 4, 64, width), jnp.bfloat16),
            pltpu.VMEM((2, transitions.shape[1]), jnp.float32),
            pltpu.VMEM((2, 2, width, width), jnp.float32),
        ),
        in_specs=[pl.BlockSpec(memory_space=pltpu.HBM)] * 5,
        out_specs=[vmem] * 4,
        scratch_shapes=[
            pltpu.VMEM(pair_elements.shape, jnp.bfloat16),
            pltpu.VMEM(transitions.shape, jnp.int32),
            pltpu.VMEM(energies.shape, jnp.float32),
            pltpu.VMEM(occupations.shape, jnp.int32),
            pltpu.SMEM(frequencies.shape, jnp.float32),
            dma((5,)), dma, dma((4,)), dma((4,)), dma((4,)), dma((64,)), dma((10,)), dma((10,)), dma((8,)), dma((8,)),
        ],
        compiler_params=pltpu.CompilerParams(
            collective_id=0, has_side_effects=True, vmem_limit_bytes=8 * 2**20
        ),
    )(*inputs)
    return pl.pallas_call(
        finish_kernel,
        out_shape=jax.ShapeDtypeStruct((2, 2, width, width), jnp.float32),
        in_specs=[vmem] * 4,
        out_specs=pl.BlockSpec(memory_space=pl.ANY),
        scratch_shapes=[pltpu.VMEM((2, 2, width, width), jnp.float32), dma((width // TILE, 2, 2))],
        compiler_params=pltpu.CompilerParams(vmem_limit_bytes=24 * 2**20),
    )(*kept)


def solution(mesh):
    in_specs = (P(None, ("row", "freq"), "col"), P(), P(), P(), P("freq"))
    out_specs = P("freq", None, "row", "col")
    return jax.shard_map(body, mesh=mesh, in_specs=in_specs, out_specs=out_specs, check_vma=False)
```
